32 devices in a mesh: tm: 8 (over y, x, core), band: 4 (over z).
Axes of the slice: x: 2, y: 2, z: 4, core: 2. Of those that a mesh axis runs over, the one named last changes fastest.
Arguments:
- voltages: bfloat16 [4, 2, 1024, 16384], P('band', None, None, 'tm'), may hold values from -6 to 6
- antenna_flags: int32 [4, 64, 1024], P('band', 'tm'), may hold values from 0 to 1, as said below
- channel_flags: int32 [4, 64], P('band', 'tm'), may hold values from 0 to 1, as said below
Outputs:
- running_vis: float32 [4, 8, 1024, 1024], P('band', 'tm')
- dump_vis: float32 [4, 1024, 1024], P('band', 'tm')
- kurtosis: float32 [4, 1024], P('band', 'tm')
The draws below stay inside these ranges and needn't reach their ends.
Inputs may be any that keep to these rules, and one draw needn't show every extreme that they name: `antenna_flags`: in the first flag interval of every segment of 8 intervals no signal input is dropped. `channel_flags`: every channel is kept in the first flag interval of at least one segment.
All inputs are finite; a program needn't handle non-finite values.
Results may differ from the reference program's by a relative error of at most 0.0003.
Values sent between devices are 32-bit elements; how exact they have to be, the bound alone decides.
A program may use at most 192 MiB of HBM per device.

```python
import jax
import jax.numpy as jnp
from jax import lax

S = 1024
TS = 2048
SEGLEN = 256
SEG_DEV = 8
NB = 4
NSEG = 64
TSAMP = 16384
N_TM = 8
N_BAND = 4


def draw_antenna_flags(key, part):
    drawn = jax.random.randint(key, (NB, NSEG, S), 0, 8)
    interval = jnp.arange(NSEG, dtype=jnp.int32)[None, :, None]
    forced = interval % SEG_DEV == 0
    return jnp.where(forced | (drawn > 0), 1, 0).astype(jnp.int32)


def draw_channel_flags(key, part):
    drawn = jax.random.randint(key, (NB, NSEG), 0, 4)
    chosen = jax.random.randint(jax.random.fold_in(key, 7), (NB, 1), 0, NSEG // SEG_DEV) * SEG_DEV
    interval = jnp.arange(NSEG, dtype=jnp.int32)[None, :]
    forced = interval == chosen
    return jnp.where(forced | (drawn > 0), 1, 0).astype(jnp.int32)


def shard_levels(key, dims, shards, least, largest):
    factor_of = 1.0
    for axis_at, parts in shards:
        draws = jax.random.uniform(jax.random.fold_in(jax.random.fold_in(key, 6), axis_at), (parts,), jnp.float32, least / len(shards), largest / len(shards))
        factor_of = factor_of * jnp.repeat(jnp.exp(draws), dims[axis_at] // parts).reshape((-1,) + (1,) * (len(dims) - 1 - axis_at))
    return factor_of


def scatter_about(own_key, shape, deviation, reach, pieces=(), kind=jnp.bfloat16):
    factor_of = shard_levels(own_key, shape, pieces, -0.22, 0.18) if pieces else 1.0
    values = jax.random.normal(own_key, shape, jnp.float32) * deviation * factor_of
    return jnp.minimum(jnp.maximum(values, -reach), reach).astype(kind)


def setup_inputs(seed: int = 0) -> dict:
    streams_of = jax.random.split(jax.random.key(seed), 4)
    voltages = scatter_about(streams_of[0], (NB, 2, S, TSAMP), 1.0, 6.0, ((0, 4), (3, 8)))
    antenna_flags = draw_antenna_flags(jax.random.fold_in(streams_of[3], 71), 0)
    channel_flags = draw_channel_flags(jax.random.fold_in(streams_of[3], 71), 0)
    return dict(voltages=voltages, antenna_flags=antenna_flags, channel_flags=channel_flags)


def band_terms(voltages, antenna_flags, channel_flags):
    keep_weight = (channel_flags[:, None] * antenna_flags).astype(jnp.float32)
    keep_weight = jnp.swapaxes(keep_weight, 0, 1)
    keep_weight = jnp.repeat(keep_weight, SEGLEN, axis=1)
    masked = voltages.astype(jnp.float32) * keep_weight[None]
    energy = masked[0] * masked[0] + masked[1] * masked[1]
    moment_one = jnp.sum(energy, axis=-1)
    moment_two = jnp.sum(energy * energy, axis=-1)
    valid_count = jnp.sum(keep_weight, axis=-1)
    kurtosis = (valid_count + 1.0) / (valid_count - 1.0) * (valid_count * moment_two / (moment_one * moment_one) - 1.0)
    row_ids = jnp.arange(S, dtype=jnp.int32)
    upper_half = row_ids[:, None] <= row_ids[None, :]

    def segment(integrated, segment_index):
        segment_data = lax.dynamic_slice_in_dim(masked, segment_index * TS, TS, 2)
        real_part = jnp.einsum('rst,rut->su', segment_data, segment_data, precision=lax.Precision.HIGHEST)
        cross_term = jnp.einsum('st,ut->su', segment_data[1], segment_data[0], precision=lax.Precision.HIGHEST)
        imag_part = cross_term - jnp.swapaxes(cross_term, 0, 1)
        gram_block = jnp.where(upper_half, real_part, imag_part) / TSAMP
        integrated = integrated + gram_block
        return integrated, integrated

    dump_total, running = lax.scan(segment, jnp.zeros((S, S), jnp.float32), jnp.arange(N_TM, dtype=jnp.int32))
    return running, dump_total, kurtosis


def reference(voltages, antenna_flags, channel_flags):
    running_all = []
    total_all = []
    kurt_all = []
    for band_index in range(N_BAND):
        running, dump_total, kurtosis = band_terms(voltages[band_index], antenna_flags[band_index], channel_flags[band_index])
        running_all.append(running)
        total_all.append(dump_total)
        kurt_all.append(kurtosis)
    return jnp.stack(running_all), jnp.stack(total_all), jnp.stack(kurt_all)
```

```python
import functools

import jax
import jax.numpy as jnp
from jax import lax
from jax.experimental import pallas as pl
from jax.experimental.pallas import tpu as pltpu
from jax.sharding import PartitionSpec as P

MESH = pl.DeviceIdType.MESH
STEPS = 32


def chain_kernel(
    n, gram, stats, run_out, dump_out, kurt_out,
    partner, earlier, first, second, stats_in,
    x_send, x_recv, c_send, c_recv, p_send, p_recv, o_sem, d_send, d_recv, s_send, s_recv,
):
    me = lax.axis_index("tm")
    chips = n // 2
    chip, core = me // 2, me % 2
    other = chip * 2 + (1 - core)
    rows = gram.shape[0] // n
    step_rows = chips * rows // STEPS
    per_slab = rows // step_rows
    last = chips - 1

    def at(q, parity):
        slab, part = q // per_slab, q % per_slab
        return pl.ds(pl.multiple_of((slab * 2 + parity) * rows + part * step_rows, 8), step_rows)

    def flat(q):
        return pl.ds(pl.multiple_of(q * step_rows, 8), step_rows)

    def exchange(q):
        return pltpu.make_async_remote_copy(
            gram.at[at(q, 1 - core)], partner.at[flat(q)], x_send.at[q], x_recv.at[q],
            device_id={"tm": other}, device_id_type=MESH)

    def onward(q, to):
        return pltpu.make_async_remote_copy(
            second.at[flat(q)], earlier.at[flat(q)], c_send.at[q], c_recv.at[q],
            device_id={"tm": to}, device_id_type=MESH)

    def hand_over(q, source, parity):
        return pltpu.make_async_remote_copy(
            source.at[flat(q)], run_out.at[at(q, parity)], p_send.at[q], p_recv.at[q],
            device_id={"tm": other}, device_id_type=MESH)

    def keep_own(q, source):
        return pltpu.make_async_copy(source.at[flat(q)], run_out.at[at(q, core)], o_sem.at[q])

    def dump_rows(q):
        return pl.ds(pl.multiple_of((q % per_slab) * step_rows, 8), step_rows)

    def dump_send(q):
        return pltpu.make_async_remote_copy(
            second.at[flat(q)], dump_out.at[dump_rows(q)], d_send.at[q], d_recv.at[q % per_slab],
            device_id={"tm": (q // per_slab) * 2 + core}, device_id_type=MESH)

    def dump_keep(q):
        return pltpu.make_async_copy(second.at[flat(q)], dump_out.at[dump_rows(q)], d_send.at[q])

    def stat_copy(o):
        to = lax.rem(me + o, n)
        return pltpu.make_async_remote_copy(
            stats.at[to], stats_in.at[o], s_send.at[o], s_recv.at[o],
            device_id={"tm": to}, device_id_type=MESH)

    barrier = pltpu.get_barrier_semaphore()
    for o in range(1, n):
        pl.semaphore_signal(barrier, inc=1, device_id={"tm": lax.rem(me + o, n)}, device_id_type=MESH)
    pl.semaphore_wait(barrier, n - 1)

    @pl.loop(0, STEPS)
    def _(q):
        exchange(q).start()

    for o in range(1, n):
        stat_copy(o).start()

    @pl.loop(0, STEPS)
    def _(q):
        exchange(q).wait_recv()
        mine = gram[at(q, core)]
        theirs = partner[flat(q)]
        low = jnp.where(core == 0, mine, theirs)

        @pl.when(chip > 0)
        def _():
            onward(q, me).wait_recv()
            first[flat(q)] = earlier[flat(q)] + low

        @pl.when(chip == 0)
        def _():
            first[flat(q)] = low

        second[flat(q)] = first[flat(q)] + jnp.where(core == 0, theirs, mine)

        @pl.when(chip < last)
        def _():
            onward(q, me + 2).start()

        @pl.when(chip == last)
        def _():
            @pl.when(q // per_slab < last)
            def _():
                dump_send(q).start()

            @pl.when(q // per_slab == last)
            def _():
                dump_keep(q).start()

        @pl.when(core == 0)
        def _():
            hand_over(q, second, 0).start()
            keep_own(q, first).start()

        @pl.when(core == 1)
        def _():
            hand_over(q, first, 1).start()
            keep_own(q, second).start()

    total = stats[me]
    for o in range(1, n):
        stat_copy(o).wait_recv()
        total = total + stats_in[o]
    one, two, count = total[0:1], total[1:2], total[2:3]
    kurt_out[...] = (count + 1.0) / (count - 1.0) * (count * two / (one * one) - 1.0)
    for o in range(1, n):
        stat_copy(o).wait_send()

    @pl.loop(0, STEPS)
    def _(q):
        exchange(q).wait_send()

        @pl.when(chip < last)
        def _():
            onward(q, me + 2).wait_send()

        @pl.when(chip == last)
        def _():
            @pl.when(q // per_slab < last)
            def _():
                dump_send(q).wait_send()

            @pl.when(q // per_slab == last)
            def _():
                dump_keep(q).wait()

        hand_over(q, second, 0).wait_send()
        hand_over(q, second, 0).wait_recv()
        keep_own(q, first).wait()

    @pl.when(chip < last)
    def _():
        @pl.loop(0, per_slab)
        def _(q):
            dump_send(q).wait_recv()


def chain(gram, stats, n):
    signals = gram.shape[0]
    rows = signals // n
    half = (signals // 2, signals)
    per_slab = rows * STEPS // (signals // 2)
    dma = pltpu.SemaphoreType.DMA
    vmem = pl.BlockSpec(memory_space=pltpu.VMEM)
    hbm = pl.BlockSpec(memory_space=pl.ANY)
    return pl.pallas_call(
        functools.partial(chain_kernel, n),
        out_shape=[
            jax.ShapeDtypeStruct((signals, signals), jnp.float32),
            jax.ShapeDtypeStruct((rows, signals), jnp.float32),
            jax.ShapeDtypeStruct((1, rows), jnp.float32),
        ],
        in_specs=[vmem, vmem],
        out_specs=[hbm, hbm, vmem],
        scratch_shapes=[
            pltpu.VMEM(half, jnp.float32),
            pltpu.VMEM(half, jnp.float32),
            pltpu.VMEM(half, jnp.float32),
            pltpu.VMEM(half, jnp.float32),
            pltpu.VMEM(stats.shape, jnp.float32),
            dma((STEPS,)), dma((STEPS,)), dma((STEPS,)), dma((STEPS,)),
            dma((STEPS,)), dma((STEPS,)), dma((STEPS,)), dma((STEPS,)), dma((per_slab,)),
            dma((n,)), dma((n,)),
        ],
        compiler_params=pltpu.CompilerParams(collective_id=0, has_side_effects=True),
    )(gram, stats)


def per_device(voltages, antenna_flags, channel_flags):
    n = lax.axis_size("tm")
    local_volts = voltages[0]
    _, signals, samples = local_volts.shape
    intervals = antenna_flags.shape[1]
    segment_length = samples // intervals
    total_samples = samples * n
    keep_weight = channel_flags[0][:, None] * antenna_flags[0]
    keep_weight = jnp.swapaxes(keep_weight, 0, 1)
    shaped = local_volts.reshape(2, signals, intervals, segment_length)
    masked = (shaped * keep_weight[None, :, :, None].astype(jnp.bfloat16)).reshape(
        2, signals, samples
    )
    real_part = jnp.einsum("rst,rut->su", masked, masked, preferred_element_type=jnp.float32)
    cross_term = jnp.einsum("st,ut->su", masked[1], masked[0], preferred_element_type=jnp.float32)
    imag_part = cross_term - jnp.swapaxes(cross_term, 0, 1)
    row_ids = jnp.arange(signals, dtype=jnp.int32)
    upper_half = row_ids[:, None] <= row_ids[None, :]
    gram_block = jnp.where(upper_half, real_part, imag_part) / total_samples
    real_volts = masked[0].astype(jnp.float32)
    imag_volts = masked[1].astype(jnp.float32)
    energy = real_volts * real_volts + imag_volts * imag_volts
    moment_one = jnp.sum(energy, axis=-1)
    moment_two = jnp.sum(energy * energy, axis=-1)
    valid_count = jnp.sum(keep_weight.astype(jnp.float32), axis=-1) * segment_length
    stats = jnp.stack([moment_one, moment_two, valid_count]).reshape(3, n, signals // n)
    stats = jnp.pad(jnp.swapaxes(stats, 0, 1), ((0, 0), (0, 5), (0, 0)))
    running, dump_rows, kurtosis = chain(gram_block, stats, n)
    return (running[None, None], dump_rows[None], kurtosis)


def solution(mesh):
    return jax.shard_map(
        per_device,
        mesh=mesh,
        in_specs=(P("band", None, None, "tm"), P("band", "tm", None), P("band", "tm")),
        out_specs=(P("band", "tm", None, None), P("band", "tm", None), P("band", "tm")),
        check_vma=False,
    )
```

```python
import functools

import jax
import jax.numpy as jnp
from jax import lax
from jax.experimental import pallas as pl
from jax.experimental.pallas import tpu as pltpu
from jax.sharding import PartitionSpec as P

MESH = pl.DeviceIdType.MESH
STEPS = 32


def chain_kernel(
    n, volts, antenna, channel, run_out, dump_out, kurt_out,
    x, keep, gram, stats, partner, earlier, first, second, stats_in,
    load, x_send, x_recv, c_send, c_recv, p_send, p_recv, o_sem, d_send, d_recv, s_send, s_recv,
):
    me = lax.axis_index("tm")
    chips = n // 2
    chip, core = me // 2, me % 2
    other = chip * 2 + (1 - core)
    rows = gram.shape[0] // n
    step_rows = chips * rows // STEPS
    per_slab = rows // step_rows
    last = chips - 1
    _, signals, samples = x.shape
    intervals = antenna.shape[0]
    length = samples // intervals
    pair = 2 * rows
    block = stats.shape[2]
    blocks = signals // block
    share = block // rows
    early = per_slab // 2
    pieces = chips // early

    def fetch(b):
        part = (slice(None), pl.ds(pl.multiple_of(b * block, block), block))
        return pltpu.make_async_copy(volts.at[part], x.at[part], load.at[b])

    def mask_block(b):
        here = pl.ds(pl.multiple_of(b * block, block), block)
        columns = jnp.transpose(keep[:, here])
        for i in range(intervals):
            times = pl.ds(i * length, length)
            weight = jnp.broadcast_to(columns[:, i : i + 1], (block, length)).astype(x.dtype)
            for part in range(2):
                x[part, here, times] = x[part, here, times] * weight

    def product(a, a_rows, b, b_rows):
        return lax.dot_general(
            x[a, a_rows], x[b, b_rows], (((1,), (1,)), ((), ())),
            preferred_element_type=jnp.float32)

    def gram_piece(r, c):
        left = pl.ds(pl.multiple_of(r * pair, pair), pair)
        right = pl.ds(pl.multiple_of(c * pair, pair), pair)
        scale = 1.0 / (samples * n)

        def real():
            return (product(0, left, 0, right) + product(1, left, 1, right)) * scale

        def imag():
            return (product(1, left, 0, right) - product(0, left, 1, right)) * scale

        @pl.when(c > r)
        def _():
            gram[left, right] = real()

        @pl.when(c < r)
        def _():
            gram[left, right] = imag()

        @pl.when(c == r)
        def _():
            row = lax.broadcasted_iota(jnp.int32, (pair, pair), 0)
            column = lax.broadcasted_iota(jnp.int32, (pair, pair), 1)
            gram[left, right] = jnp.where(row <= column, real(), imag())

    def moments(b):
        here = pl.ds(pl.multiple_of(b * block, block), block)
        one = jnp.zeros((block, 128), jnp.float32)
        two = jnp.zeros((block, 128), jnp.float32)
        for t in range(samples // 128):
            real = x[0, here, pl.ds(t * 128, 128)].astype(jnp.float32)
            imag = x[1, here, pl.ds(t * 128, 128)].astype(jnp.float32)
            energy = real * real + imag * imag
            one = one + energy
            two = two + energy * energy
        stats[b, 0:1] = jnp.sum(jnp.transpose(one), axis=0, keepdims=True)
        stats[b, 1:2] = jnp.sum(jnp.transpose(two), axis=0, keepdims=True)
        stats[b, 2:3] = jnp.sum(keep[:, here], axis=0, keepdims=True) * length

    def at(q, parity):
        slab, part = q // per_slab, q % per_slab
        return pl.ds(pl.multiple_of((slab * 2 + parity) * rows + part * step_rows, 8), step_rows)

    def flat(q):
        return pl.ds(pl.multiple_of(q * step_rows, 8), step_rows)

    def exchange(q):
        return pltpu.make_async_remote_copy(
            gram.at[at(q, 1 - core)], partner.at[flat(q)], x_send.at[q], x_recv.at[q],
            device_id={"tm": other}, device_id_type=MESH)

    def onward(q, to):
        return pltpu.make_async_remote_copy(
            second.at[flat(q)], earlier.at[flat(q)], c_send.at[q], c_recv.at[q],
            device_id={"tm": to}, device_id_type=MESH)

    def hand_over(q, source, parity):
        return pltpu.make_async_remote_copy(
            source.at[flat(q)], run_out.at[at(q, parity)], p_send.at[q], p_recv.at[q],
            device_id={"tm": other}, device_id_type=MESH)

    def keep_own(q, source):
        return pltpu.make_async_copy(source.at[flat(q)], run_out.at[at(q, core)], o_sem.at[q])

    def dump_rows(q):
        return pl.ds(pl.multiple_of((q % per_slab) * step_rows, 8), step_rows)

    def dump_send(q):
        return pltpu.make_async_remote_copy(
            second.at[flat(q)], dump_out.at[dump_rows(q)], d_send.at[q], d_recv.at[q % per_slab],
            device_id={"tm": (q // per_slab) * 2 + core}, device_id_type=MESH)

    def dump_keep(q):
        return pltpu.make_async_copy(second.at[flat(q)], dump_out.at[dump_rows(q)], d_send.at[q])

    def stat_copy(o):
        to = lax.rem(me + o, n)
        return pltpu.make_async_remote_copy(
            stats.at[to // share], stats_in.at[o], s_send.at[o], s_recv.at[o],
            device_id={"tm": to}, device_id_type=MESH)

    barrier = pltpu.get_barrier_semaphore()
    for o in range(1, n):
        pl.semaphore_signal(barrier, inc=1, device_id={"tm": lax.rem(me + o, n)}, device_id_type=MESH)

    @pl.loop(0, blocks)
    def _(b):
        fetch(b).start()

    keep[...] = (antenna[...] * channel[...]).astype(jnp.float32)
    stats[...] = jnp.zeros_like(stats)

    @pl.loop(0, blocks)
    def _(b):
        fetch(b).wait()
        mask_block(b)

    @pl.loop(0, chips)
    def _(c):
        gram_piece(0, c)

    pl.semaphore_wait(barrier, n - 1)

    @pl.loop(0, per_slab)
    def _(q):
        exchange(q).start()

    @pl.loop(0, STEPS)
    def _(q):
        exchange(q).wait_recv()
        mine = gram[at(q, core)]
        theirs = partner[flat(q)]
        low = jnp.where(core == 0, mine, theirs)

        @pl.when(chip > 0)
        def _():
            onward(q, me).wait_recv()
            first[flat(q)] = earlier[flat(q)] + low

        @pl.when(chip == 0)
        def _():
            first[flat(q)] = low

        second[flat(q)] = first[flat(q)] + jnp.where(core == 0, theirs, mine)

        @pl.when(chip < last)
        def _():
            onward(q, me + 2).start()

        @pl.when(chip == last)
        def _():
            @pl.when(q // per_slab < last)
            def _():
                dump_send(q).start()

            @pl.when(q // per_slab == last)
            def _():
                dump_keep(q).start()

        @pl.when(core == 0)
        def _():
            hand_over(q, second, 0).start()
            keep_own(q, first).start()

        @pl.when(core == 1)
        def _():
            hand_over(q, first, 1).start()
            keep_own(q, second).start()

        slab, part = q // per_slab, q % per_slab

        @pl.when((slab < last) & (part < early))
        def _():
            @pl.loop(0, pieces)
            def _(c):
                gram_piece(slab + 1, part * pieces + c)

            @pl.when(part == early - 1)
            def _():
                @pl.loop(0, per_slab)
                def _(k):
                    exchange((slab + 1) * per_slab + k).start()

        turn = slab * early + part - early

        @pl.when((part >= early) & (turn < blocks))
        def _():
            moments(turn)

            @pl.when(turn == blocks - 1)
            def _():
                for o in range(1, n):
                    stat_copy(o).start()

    total = stats[me // share]
    for o in range(1, n):
        stat_copy(o).wait_recv()
        total = total + stats_in[o]
    mine = total[:, 0:rows]
    for k in range(1, share):
        mine = jnp.where(me % share == k, total[:, k * rows : (k + 1) * rows], mine)
    total = mine
    one, two, count = total[0:1], total[1:2], total[2:3]
    kurt_out[...] = (count + 1.0) / (count - 1.0) * (count * two / (one * one) - 1.0)
    for o in range(1, n):
        stat_copy(o).wait_send()

    @pl.loop(0, STEPS)
    def _(q):
        exchange(q).wait_send()

        @pl.when(chip < last)
        def _():
            onward(q, me + 2).wait_send()

        @pl.when(chip == last)
        def _():
            @pl.when(q // per_slab < last)
            def _():
                dump_send(q).wait_send()

            @pl.when(q // per_slab == last)
            def _():
                dump_keep(q).wait()

        hand_over(q, second, 0).wait_send()
        hand_over(q, second, 0).wait_recv()
        keep_own(q, first).wait()

    @pl.when(chip < last)
    def _():
        @pl.loop(0, per_slab)
        def _(q):
            dump_send(q).wait_recv()


def chain(volts, antenna, channel, n):
    _, signals, samples = volts.shape
    intervals = antenna.shape[0]
    rows = signals // n
    block = max(rows, 128)
    half = (signals // 2, signals)
    per_slab = rows * STEPS // (signals // 2)
    dma = pltpu.SemaphoreType.DMA
    vmem = pl.BlockSpec(memory_space=pltpu.VMEM)
    hbm = pl.BlockSpec(memory_space=pl.ANY)
    return pl.pallas_call(
        functools.partial(chain_kernel, n),
        out_shape=[
            jax.ShapeDtypeStruct((signals, signals), jnp.float32),
            jax.ShapeDtypeStruct((rows, signals), jnp.float32),
            jax.ShapeDtypeStruct((1, rows), jnp.float32),
        ],
        in_specs=[hbm, vmem, vmem],
        out_specs=[hbm, hbm, vmem],
        scratch_shapes=[
            pltpu.VMEM(volts.shape, volts.dtype),
            pltpu.VMEM((intervals, signals), jnp.float32),
            pltpu.VMEM((signals, signals), jnp.float32),
            pltpu.VMEM((signals // block, 8, block), jnp.float32),
            pltpu.VMEM(half, jnp.float32),
            pltpu.VMEM(half, jnp.float32),
            pltpu.VMEM(half, jnp.float32),
            pltpu.VMEM(half, jnp.float32),
            pltpu.VMEM((n, 8, block), jnp.float32),
            dma((signals // block,)),
            dma((STEPS,)), dma((STEPS,)), dma((STEPS,)), dma((STEPS,)),
            dma((STEPS,)), dma((STEPS,)), dma((STEPS,)), dma((STEPS,)), dma((per_slab,)),
            dma((n,)), dma((n,)),
        ],
        compiler_params=pltpu.CompilerParams(collective_id=0, has_side_effects=True),
    )(volts, antenna, channel)


def per_device(voltages, antenna_flags, channel_flags):
    n = lax.axis_size("tm")
    running, dump_rows, kurtosis = chain(
        voltages[0], antenna_flags[0], channel_flags[0][:, None], n
    )
    return (running[None, None], dump_rows[None], kurtosis)


def solution(mesh):
    return jax.shard_map(
        per_device,
        mesh=mesh,
        in_specs=(P("band", None, None, "tm"), P("band", "tm", None), P("band", "tm")),
        out_specs=(P("band", "tm", None, None), P("band", "tm", None), P("band", "tm")),
        check_vma=False,
    )
```

```python
import functools

import jax
import jax.numpy as jnp
from jax import lax
from jax.experimental import pallas as pl
from jax.experimental.pallas import tpu as pltpu
from jax.sharding import PartitionSpec as P

MESH = pl.DeviceIdType.MESH
STEPS = 32
VMEM_BYTES = 57 * 2**20


def chain_kernel(
    n, volts, antenna, channel, run_out, dump_out, kurt_out,
    x, keep, gram, stats, partner, earlier, first, second, stats_in,
    load, x_send, x_recv, c_send, c_recv, p_send, p_recv, o_sem, d_send, d_recv, s_send, s_recv,
):
    me = lax.axis_index("tm")
    chips = n // 2
    chip, core = me // 2, me % 2
    other = chip * 2 + (1 - core)
    rows = gram.shape[0] // n
    per_slab = STEPS // chips
    width = gram.shape[0] // per_slab
    last = chips - 1
    _, signals, samples = x.shape
    intervals = antenna.shape[0]
    length = samples // intervals
    pair = 2 * rows
    block = stats.shape[2]
    blocks = signals // block
    share = block // rows
    wide = max(pair, width)
    pieces = signals // wide
    steps = chips * pieces
    chunks = wide // width

    def fetch(b):
        part = (slice(None), pl.ds(pl.multiple_of(b * block, block), block))
        return pltpu.make_async_copy(volts.at[part], x.at[part], load.at[b])

    def mask_block(b):
        here = pl.ds(pl.multiple_of(b * block, block), block)
        kept = jnp.transpose(keep[:, here])
        for i in range(intervals):
            times = pl.ds(i * length, length)
            weight = jnp.broadcast_to(kept[:, i : i + 1], (block, length)).astype(x.dtype)
            for part in range(2):
                x[part, here, times] = x[part, here, times] * weight

    def product(a, a_rows, b, b_rows):
        return lax.dot_general(
            x[a, a_rows], x[b, b_rows], (((1,), (1,)), ((), ())),
            preferred_element_type=jnp.float32)

    def gram_piece(r, c):
        left = pl.ds(pl.multiple_of(r * pair, pair), pair)
        right = pl.ds(pl.multiple_of(c * wide, wide), wide)
        scale = 1.0 / (samples * n)

        def real():
            return (product(0, left, 0, right) + product(1, left, 1, right)) * scale

        def imag():
            return (product(1, left, 0, right) - product(0, left, 1, right)) * scale

        above = c * wide >= (r + 1) * pair
        below = (c + 1) * wide <= r * pair

        @pl.when(above)
        def _():
            gram[left, right] = real()

        @pl.when(below)
        def _():
            gram[left, right] = imag()

        @pl.when(jnp.logical_not(above | below))
        def _():
            row = lax.broadcasted_iota(jnp.int32, (pair, wide), 0) + r * pair
            column = lax.broadcasted_iota(jnp.int32, (pair, wide), 1) + c * wide
            gram[left, right] = jnp.where(row <= column, real(), imag())

    def moments(b):
        here = pl.ds(pl.multiple_of(b * block, block), block)
        one = jnp.zeros((block, 128), jnp.float32)
        two = jnp.zeros((block, 128), jnp.float32)
        for t in range(samples // 128):
            real = x[0, here, pl.ds(t * 128, 128)].astype(jnp.float32)
            imag = x[1, here, pl.ds(t * 128, 128)].astype(jnp.float32)
            energy = real * real + imag * imag
            one = one + energy
            two = two + energy * energy
        stats[b, 0:1] = jnp.sum(jnp.transpose(one), axis=0, keepdims=True)
        stats[b, 1:2] = jnp.sum(jnp.transpose(two), axis=0, keepdims=True)
        stats[b, 2:3] = jnp.sum(keep[:, here], axis=0, keepdims=True) * length

    def columns(q):
        return pl.ds(pl.multiple_of((q % per_slab) * width, width), width)

    def at(q, parity):
        first_row = ((q // per_slab) * 2 + parity) * rows
        return (pl.ds(pl.multiple_of(first_row, rows), rows), columns(q))

    def exchange(q):
        return pltpu.make_async_remote_copy(
            gram.at[at(q, 1 - core)], partner.at[q], x_send.at[q], x_recv.at[q],
            device_id={"tm": other}, device_id_type=MESH)

    def onward(q, to):
        return pltpu.make_async_remote_copy(
            second.at[q], earlier.at[q], c_send.at[q], c_recv.at[q],
            device_id={"tm": to}, device_id_type=MESH)

    def hand_over(q, source, parity):
        return pltpu.make_async_remote_copy(
            source.at[q], run_out.at[at(q, parity)], p_send.at[q], p_recv.at[q],
            device_id={"tm": other}, device_id_type=MESH)

    def keep_own(q, source):
        return pltpu.make_async_copy(source.at[q], run_out.at[at(q, core)], o_sem.at[q])

    def dump_send(q):
        return pltpu.make_async_remote_copy(
            second.at[q], dump_out.at[:, columns(q)], d_send.at[q], d_recv.at[q % per_slab],
            device_id={"tm": (q // per_slab) * 2 + core}, device_id_type=MESH)

    def dump_keep(q):
        return pltpu.make_async_copy(second.at[q], dump_out.at[:, columns(q)], d_send.at[q])

    def stat_copy(o):
        to = lax.rem(me + o, n)
        return pltpu.make_async_remote_copy(
            stats.at[to // share], stats_in.at[o], s_send.at[o], s_recv.at[o],
            device_id={"tm": to}, device_id_type=MESH)

    barrier = pltpu.get_barrier_semaphore()
    for o in range(1, n):
        pl.semaphore_signal(barrier, inc=1, device_id={"tm": lax.rem(me + o, n)}, device_id_type=MESH)

    @pl.loop(0, blocks)
    def _(b):
        fetch(b).start()

    for i in range(intervals):
        keep[i : i + 1] = (antenna[i : i + 1] * channel[0, i]).astype(jnp.float32)
    stats[...] = jnp.zeros_like(stats)

    pl.semaphore_wait(barrier, n - 1)

    def advance(q):
        exchange(q).wait_recv()
        mine = gram[at(q, core)]
        theirs = partner[q]
        low = jnp.where(core == 0, mine, theirs)

        @pl.when(chip > 0)
        def _():
            onward(q, me).wait_recv()
            first[q] = earlier[q] + low

        @pl.when(chip == 0)
        def _():
            first[q] = low

        second[q] = first[q] + jnp.where(core == 0, theirs, mine)

        @pl.when(chip < last)
        def _():
            onward(q, me + 2).start()

        @pl.when(chip == last)
        def _():
            @pl.when(q // per_slab < last)
            def _():
                dump_send(q).start()

            @pl.when(q // per_slab == last)
            def _():
                dump_keep(q).start()

        @pl.when(core == 0)
        def _():
            hand_over(q, second, 0).start()
            keep_own(q, first).start()

        @pl.when(core == 1)
        def _():
            hand_over(q, first, 1).start()
            keep_own(q, second).start()

    @pl.loop(0, steps + 1)
    def _(g):
        @pl.when(g < pieces)
        def _():
            for k in range(wide // block):
                fetch(g * (wide // block) + k).wait()
                mask_block(g * (wide // block) + k)

        @pl.when(g < steps)
        def _():
            gram_piece(g // pieces, g % pieces)
            for k in range(chunks):
                exchange(g * chunks + k).start()

        @pl.when(g > 0)
        def _():
            @pl.loop(0, chunks)
            def _(k):
                advance((g - 1) * chunks + k)

        turn = g - pieces

        @pl.when((turn >= 0) & (turn < blocks))
        def _():
            moments(turn)

            @pl.when(turn == blocks - 1)
            def _():
                for o in range(1, n):
                    stat_copy(o).start()

    total = stats[me // share]
    for o in range(1, n):
        stat_copy(o).wait_recv()
        total = total + stats_in[o]
    mine = total[:, 0:rows]
    for k in range(1, share):
        mine = jnp.where(me % share == k, total[:, k * rows : (k + 1) * rows], mine)
    total = mine
    one, two, count = total[0:1], total[1:2], total[2:3]
    kurt_out[...] = (count + 1.0) / (count - 1.0) * (count * two / (one * one) - 1.0)
    for o in range(1, n):
        stat_copy(o).wait_send()

    @pl.loop(0, STEPS)
    def _(q):
        exchange(q).wait_send()

        @pl.when(chip < last)
        def _():
            onward(q, me + 2).wait_send()

        @pl.when(chip == last)
        def _():
            @pl.when(q // per_slab < last)
            def _():
                dump_send(q).wait_send()

            @pl.when(q // per_slab == last)
            def _():
                dump_keep(q).wait()

        hand_over(q, second, 0).wait_send()
        hand_over(q, second, 0).wait_recv()
        keep_own(q, first).wait()

    @pl.when(chip < last)
    def _():
        @pl.loop(0, per_slab)
        def _(q):
            dump_send(q).wait_recv()


def chain(volts, antenna, channel, n):
    _, signals, samples = volts.shape
    intervals = antenna.shape[0]
    rows = signals // n
    block = max(rows, 128)
    per_slab = STEPS // (n // 2)
    half = (STEPS, rows, signals // per_slab)
    dma = pltpu.SemaphoreType.DMA
    vmem = pl.BlockSpec(memory_space=pltpu.VMEM)
    hbm = pl.BlockSpec(memory_space=pl.ANY)
    return pl.pallas_call(
        functools.partial(chain_kernel, n),
        out_shape=[
            jax.ShapeDtypeStruct((signals, signals), jnp.float32),
            jax.ShapeDtypeStruct((rows, signals), jnp.float32),
            jax.ShapeDtypeStruct((1, rows), jnp.float32),
        ],
        in_specs=[
            pl.BlockSpec(memory_space=pltpu.HBM),
            vmem,
            pl.BlockSpec(memory_space=pltpu.SMEM),
        ],
        out_specs=[hbm, hbm, vmem],
        scratch_shapes=[
            pltpu.VMEM(volts.shape, volts.dtype),
            pltpu.VMEM((intervals, signals), jnp.float32),
            pltpu.VMEM((signals, signals), jnp.float32),
            pltpu.VMEM((signals // block, 8, block), jnp.float32),
            pltpu.VMEM(half, jnp.float32),
            pltpu.VMEM(half, jnp.float32),
            pltpu.VMEM(half, jnp.float32),
            pltpu.VMEM(half, jnp.float32),
            pltpu.VMEM((n, 8, block), jnp.float32),
            dma((signals // block,)),
            dma((STEPS,)), dma((STEPS,)), dma((STEPS,)), dma((STEPS,)),
            dma((STEPS,)), dma((STEPS,)), dma((STEPS,)), dma((STEPS,)), dma((per_slab,)),
            dma((n,)), dma((n,)),
        ],
        compiler_params=pltpu.CompilerParams(
            collective_id=0, has_side_effects=True, vmem_limit_bytes=VMEM_BYTES
        ),
    )(volts, antenna, channel)


def per_device(voltages, antenna_flags, channel_flags):
    n = lax.axis_size("tm")
    running, dump_rows, kurtosis = chain(
        voltages[0], antenna_flags[0], channel_flags, n
    )
    return (running[None, None], dump_rows[None], kurtosis)


def solution(mesh):
    return jax.shard_map(
        per_device,
        mesh=mesh,
        in_specs=(P("band", None, None, "tm"), P("band", "tm", None), P("band", "tm")),
        out_specs=(P("band", "tm", None, None), P("band", "tm", None), P("band", "tm")),
        check_vma=False,
    )
```

```python
import functools

import jax
import jax.numpy as jnp
from jax import lax
from jax.experimental import pallas as pl
from jax.experimental.pallas import tpu as pltpu
from jax.sharding import PartitionSpec as P

MESH = pl.DeviceIdType.MESH
STEPS = 32
LAG = 3
VMEM_BYTES = 46 * 2**20


def chain_kernel(
    n, volts, antenna, channel, run_out, dump_out, kurt_out,
    x, keep, gram, stats, partner, raw, sibling, earlier, first, second, stats_in,
    load, x_send, x_recv, r_send, r_recv, c_send, v_send, c_recv, p_send, p_recv, o_sem, d_send, d_recv, s_send, s_recv,
):
    me = lax.axis_index("tm")
    chips = n // 2
    chip, core = me // 2, me % 2
    other = chip * 2 + (1 - core)
    rows = gram.shape[0] // n
    per_slab = STEPS // chips
    width = gram.shape[0] // per_slab
    last = chips - 1
    even = chip % 2 == 0
    lag = jnp.where(even & (chip > 0), LAG, 0)
    _, signals, samples = x.shape
    intervals = antenna.shape[0]
    length = samples // intervals
    pair = 2 * rows
    block = stats.shape[2]
    blocks = signals // block
    share = block // rows
    wide = max(pair, width)
    pieces = signals // wide
    steps = chips * pieces
    chunks = wide // width

    def fetch(b):
        part = (slice(None), pl.ds(pl.multiple_of(b * block, block), block))
        return pltpu.make_async_copy(volts.at[part], x.at[part], load.at[b])

    def mask_block(b):
        here = pl.ds(pl.multiple_of(b * block, block), block)
        kept = jnp.transpose(keep[:, here])
        for i in range(intervals):
            times = pl.ds(i * length, length)
            weight = jnp.broadcast_to(kept[:, i : i + 1], (block, length)).astype(x.dtype)
            for part in range(2):
                x[part, here, times] = x[part, here, times] * weight

    def product(a, a_rows, b, b_rows):
        return lax.dot_general(
            x[a, a_rows], x[b, b_rows], (((1,), (1,)), ((), ())),
            preferred_element_type=jnp.float32)

    def gram_piece(r, c):
        left = pl.ds(pl.multiple_of(r * pair, pair), pair)
        right = pl.ds(pl.multiple_of(c * wide, wide), wide)
        scale = 1.0 / (samples * n)

        def real():
            return (product(0, left, 0, right) + product(1, left, 1, right)) * scale

        def imag():
            return (product(1, left, 0, right) - product(0, left, 1, right)) * scale

        above = c * wide >= (r + 1) * pair
        below = (c + 1) * wide <= r * pair

        @pl.when(above)
        def _():
            gram[left, right] = real()

        @pl.when(below)
        def _():
            gram[left, right] = imag()

        @pl.when(jnp.logical_not(above | below))
        def _():
            row = lax.broadcasted_iota(jnp.int32, (pair, wide), 0) + r * pair
            column = lax.broadcasted_iota(jnp.int32, (pair, wide), 1) + c * wide
            gram[left, right] = jnp.where(row <= column, real(), imag())

    def moments(b):
        here = pl.ds(pl.multiple_of(b * block, block), block)
        one = jnp.zeros((block, 128), jnp.float32)
        two = jnp.zeros((block, 128), jnp.float32)
        for t in range(samples // 128):
            real = x[0, here, pl.ds(t * 128, 128)].astype(jnp.float32)
            imag = x[1, here, pl.ds(t * 128, 128)].astype(jnp.float32)
            energy = real * real + imag * imag
            one = one + energy
            two = two + energy * energy
        stats[b, 0:1] = jnp.sum(jnp.transpose(one), axis=0, keepdims=True)
        stats[b, 1:2] = jnp.sum(jnp.transpose(two), axis=0, keepdims=True)
        stats[b, 2:3] = jnp.sum(keep[:, here], axis=0, keepdims=True) * length

    def columns(q):
        return pl.ds(pl.multiple_of((q % per_slab) * width, width), width)

    def at(q, parity):
        first_row = ((q // per_slab) * 2 + parity) * rows
        return (pl.ds(pl.multiple_of(first_row, rows), rows), columns(q))

    def exchange(q):
        return pltpu.make_async_remote_copy(
            gram.at[at(q, 1 - core)], partner.at[q], x_send.at[q], x_recv.at[q],
            device_id={"tm": other}, device_id_type=MESH)

    def send_raw(q, to):
        return pltpu.make_async_remote_copy(
            raw.at[q], sibling.at[q], r_send.at[q], r_recv.at[q],
            device_id={"tm": to}, device_id_type=MESH)

    def onward(q, to, sem):
        return pltpu.make_async_remote_copy(
            second.at[q], earlier.at[q], sem.at[q], c_recv.at[q],
            device_id={"tm": to}, device_id_type=MESH)

    def hand_over(q, source, parity):
        return pltpu.make_async_remote_copy(
            source.at[q], run_out.at[at(q, parity)], p_send.at[q], p_recv.at[q],
            device_id={"tm": other}, device_id_type=MESH)

    def keep_own(q, source):
        return pltpu.make_async_copy(source.at[q], run_out.at[at(q, core)], o_sem.at[q])

    def dump_send(q):
        return pltpu.make_async_remote_copy(
            second.at[q], dump_out.at[:, columns(q)], d_send.at[q], d_recv.at[q % per_slab],
            device_id={"tm": (q // per_slab) * 2 + core}, device_id_type=MESH)

    def dump_keep(q):
        return pltpu.make_async_copy(second.at[q], dump_out.at[:, columns(q)], d_send.at[q])

    def stat_copy(o):
        to = lax.rem(me + o, n)
        return pltpu.make_async_remote_copy(
            stats.at[to // share], stats_in.at[o], s_send.at[o], s_recv.at[o],
            device_id={"tm": to}, device_id_type=MESH)

    barrier = pltpu.get_barrier_semaphore()
    for o in range(1, n):
        pl.semaphore_signal(barrier, inc=1, device_id={"tm": lax.rem(me + o, n)}, device_id_type=MESH)

    opening = wide // block
    for b in range(opening):
        fetch(b).start()

    for i in range(intervals):
        keep[i : i + 1] = (antenna[i : i + 1] * channel[0, i]).astype(jnp.float32)
    stats[...] = jnp.zeros_like(stats)

    for b in range(opening):
        fetch(b).wait()

    @pl.loop(opening, blocks)
    def _(b):
        fetch(b).start()

    for b in range(opening):
        mask_block(b)
    gram_piece(0, 0)

    pl.semaphore_wait(barrier, n - 1)

    def gather(q):
        exchange(q).wait_recv()

        @pl.when(even)
        def _():
            raw[q] = gram[at(q, core)] + partner[q]
            send_raw(q, me + 2).start()

    def advance(q):
        mine = gram[at(q, core)]
        theirs = partner[q]
        low = jnp.where(core == 0, mine, theirs)
        first[q] = low

        @pl.when(chip > 1)
        def _():
            onward(q, me, c_send).wait_recv()
            first[q] = first[q] + earlier[q]

        @pl.when(jnp.logical_not(even))
        def _():
            send_raw(q, me).wait_recv()
            first[q] = first[q] + sibling[q]

        second[q] = first[q] + jnp.where(core == 0, theirs, mine)

        @pl.when(jnp.logical_not(even) & (chip < last))
        def _():
            onward(q, me + 4, v_send).start()
            onward(q, me + 2, c_send).start()

        @pl.when(chip == last)
        def _():
            @pl.when(q // per_slab < last)
            def _():
                dump_send(q).start()

            @pl.when(q // per_slab == last)
            def _():
                dump_keep(q).start()

        @pl.when(core == 0)
        def _():
            hand_over(q, second, 0).start()
            keep_own(q, first).start()

        @pl.when(core == 1)
        def _():
            hand_over(q, first, 1).start()
            keep_own(q, second).start()

    @pl.loop(0, steps + 1 + LAG)
    def _(g):
        @pl.when((g > 0) & (g < pieces))
        def _():
            for k in range(opening):
                fetch(g * opening + k).wait()
                mask_block(g * opening + k)

        @pl.when(g < steps)
        def _():
            @pl.when(g > 0)
            def _():
                gram_piece(g // pieces, g % pieces)

            for k in range(chunks):
                exchange(g * chunks + k).start()

        @pl.when((g > 0) & (g <= steps))
        def _():
            @pl.loop(0, chunks)
            def _(k):
                gather((g - 1) * chunks + k)

        due = g - 1 - lag

        @pl.when((due >= 0) & (due < steps))
        def _():
            @pl.loop(0, chunks)
            def _(k):
                advance(due * chunks + k)

        turn = g - pieces

        @pl.when((turn >= 0) & (turn < blocks))
        def _():
            moments(turn)

            @pl.when(turn == blocks - 1)
            def _():
                for o in range(1, n):
                    stat_copy(o).start()

    total = stats[me // share]
    for o in range(1, n):
        stat_copy(o).wait_recv()
        total = total + stats_in[o]
    mine = total[:, 0:rows]
    for k in range(1, share):
        mine = jnp.where(me % share == k, total[:, k * rows : (k + 1) * rows], mine)
    total = mine
    one, two, count = total[0:1], total[1:2], total[2:3]
    kurt_out[...] = (count + 1.0) / (count - 1.0) * (count * two / (one * one) - 1.0)
    for o in range(1, n):
        stat_copy(o).wait_send()

    @pl.loop(0, STEPS)
    def _(q):
        exchange(q).wait_send()

        @pl.when(even)
        def _():
            send_raw(q, me + 2).wait_send()

        @pl.when(jnp.logical_not(even) & (chip < last))
        def _():
            onward(q, me + 4, v_send).wait_send()
            onward(q, me + 2, c_send).wait_send()

        @pl.when(chip == last)
        def _():
            @pl.when(q // per_slab < last)
            def _():
                dump_send(q).wait_send()

            @pl.when(q // per_slab == last)
            def _():
                dump_keep(q).wait()

        hand_over(q, second, 0).wait_send()
        hand_over(q, second, 0).wait_recv()
        keep_own(q, first).wait()

    @pl.when(chip < last)
    def _():
        @pl.loop(0, per_slab)
        def _(q):
            dump_send(q).wait_recv()


def chain(volts, antenna, channel, n):
    _, signals, samples = volts.shape
    intervals = antenna.shape[0]
    rows = signals // n
    block = max(rows, 128)
    per_slab = STEPS // (n // 2)
    half = (STEPS, rows, signals // per_slab)
    dma = pltpu.SemaphoreType.DMA
    vmem = pl.BlockSpec(memory_space=pltpu.VMEM)
    hbm = pl.BlockSpec(memory_space=pl.ANY)
    return pl.pallas_call(
        functools.partial(chain_kernel, n),
        out_shape=[
            jax.ShapeDtypeStruct((signals, signals), jnp.float32),
            jax.ShapeDtypeStruct((rows, signals), jnp.float32),
            jax.ShapeDtypeStruct((1, rows), jnp.float32),
        ],
        in_specs=[
            pl.BlockSpec(memory_space=pltpu.HBM),
            vmem,
            pl.BlockSpec(memory_space=pltpu.SMEM),
        ],
        out_specs=[hbm, hbm, vmem],
        scratch_shapes=[
            pltpu.VMEM(volts.shape, volts.dtype),
            pltpu.VMEM((intervals, signals), jnp.float32),
            pltpu.VMEM((signals, signals), jnp.float32),
            pltpu.VMEM((signals // block, 8, block), jnp.float32),
            pltpu.VMEM(half, jnp.float32),
            pltpu.VMEM(half, jnp.float32),
            pltpu.VMEM(half, jnp.float32),
            pltpu.VMEM(half, jnp.float32),
            pltpu.VMEM(half, jnp.float32),
            pltpu.VMEM(half, jnp.float32),
            pltpu.VMEM((n, 8, block), jnp.float32),
            dma((signals // block,)),
            dma((STEPS,)), dma((STEPS,)), dma((STEPS,)), dma((STEPS,)),
            dma((STEPS,)), dma((STEPS,)), dma((STEPS,)), dma((STEPS,)), dma((STEPS,)), dma((STEPS,)), dma((STEPS,)), dma((per_slab,)),
            dma((n,)), dma((n,)),
        ],
        compiler_params=pltpu.CompilerParams(
            collective_id=0, has_side_effects=True, vmem_limit_bytes=VMEM_BYTES
        ),
    )(volts, antenna, channel)


def per_device(voltages, antenna_flags, channel_flags):
    n = lax.axis_size("tm")
    running, dump_rows, kurtosis = chain(
        voltages[0], antenna_flags[0], channel_flags, n
    )
    return (running[None, None], dump_rows[None], kurtosis)


def solution(mesh):
    return jax.shard_map(
        per_device,
        mesh=mesh,
        in_specs=(P("band", None, None, "tm"), P("band", "tm", None), P("band", "tm")),
        out_specs=(P("band", "tm", None, None), P("band", "tm", None), P("band", "tm")),
        check_vma=False,
    )
```

```python
import functools

import jax
import jax.numpy as jnp
from jax import lax
from jax.experimental import pallas as pl
from jax.experimental.pallas import tpu as pltpu
from jax.sharding import PartitionSpec as P

MESH = pl.DeviceIdType.MESH
STEPS = 32
LAG = 3
VMEM_BYTES = 46 * 2**20


def chain_kernel(
    n, volts, antenna, channel, run_out, dump_out, kurt_out,
    x, keep, gram, stats, partner, raw, sibling, earlier, first, second, stats_in,
    load, x_send, x_recv, r_send, r_recv, c_send, v_send, c_recv, p_send, p_recv, o_sem, d_send, d_recv, k_sem, s_send, s_recv,
):
    me = lax.axis_index("tm")
    chips = n // 2
    chip, core = me // 2, me % 2
    other = chip * 2 + (1 - core)
    rows = gram.shape[0] // n
    per_slab = STEPS // chips
    width = gram.shape[0] // per_slab
    last = chips - 1
    even = chip % 2 == 0
    lag = jnp.where(even & (chip > 0), LAG, 0)
    _, signals, samples = x.shape
    intervals = antenna.shape[0]
    length = samples // intervals
    pair = 2 * rows
    block = stats.shape[2]
    blocks = signals // block
    share = block // rows
    wide = max(pair, width)
    pieces = signals // wide
    steps = chips * pieces
    chunks = wide // width

    def fetch(b):
        part = (slice(None), pl.ds(pl.multiple_of(b * block, block), block))
        return pltpu.make_async_copy(volts.at[part], x.at[part], load.at[b])

    def mask_block(b):
        here = pl.ds(pl.multiple_of(b * block, block), block)
        kept = jnp.transpose(keep[:, here])
        for i in range(intervals):
            times = pl.ds(i * length, length)
            weight = jnp.broadcast_to(kept[:, i : i + 1], (block, length)).astype(x.dtype)
            for part in range(2):
                x[part, here, times] = x[part, here, times] * weight

    def product(a, a_rows, b, b_rows):
        return lax.dot_general(
            x[a, a_rows], x[b, b_rows], (((1,), (1,)), ((), ())),
            preferred_element_type=jnp.float32)

    def gram_piece(r, c):
        left = pl.ds(pl.multiple_of(r * pair, pair), pair)
        right = pl.ds(pl.multiple_of(c * wide, wide), wide)
        scale = 1.0 / (samples * n)

        def real():
            return (product(0, left, 0, right) + product(1, left, 1, right)) * scale

        def imag():
            return (product(1, left, 0, right) - product(0, left, 1, right)) * scale

        above = c * wide >= (r + 1) * pair
        below = (c + 1) * wide <= r * pair

        @pl.when(above)
        def _():
            gram[left, right] = real()

        @pl.when(below)
        def _():
            gram[left, right] = imag()

        @pl.when(jnp.logical_not(above | below))
        def _():
            row = lax.broadcasted_iota(jnp.int32, (pair, wide), 0) + r * pair
            column = lax.broadcasted_iota(jnp.int32, (pair, wide), 1) + c * wide
            gram[left, right] = jnp.where(row <= column, real(), imag())

    def moments(b):
        here = pl.ds(pl.multiple_of(b * block, block), block)
        one = jnp.zeros((block, 128), jnp.float32)
        two = jnp.zeros((block, 128), jnp.float32)
        for t in range(samples // 128):
            real = x[0, here, pl.ds(t * 128, 128)].astype(jnp.float32)
            imag = x[1, here, pl.ds(t * 128, 128)].astype(jnp.float32)
            energy = real * real + imag * imag
            one = one + energy
            two = two + energy * energy
        stats[b, 0:1] = jnp.sum(jnp.transpose(one), axis=0, keepdims=True)
        stats[b, 1:2] = jnp.sum(jnp.transpose(two), axis=0, keepdims=True)
        stats[b, 2:3] = jnp.sum(keep[:, here], axis=0, keepdims=True) * length

    def columns(q):
        return pl.ds(pl.multiple_of((q % per_slab) * width, width), width)

    def at(q, parity):
        first_row = ((q // per_slab) * 2 + parity) * rows
        return (pl.ds(pl.multiple_of(first_row, rows), rows), columns(q))

    def exchange(q):
        return pltpu.make_async_remote_copy(
            gram.at[at(q, 1 - core)], partner.at[q], x_send, x_recv.at[q],
            device_id={"tm": other}, device_id_type=MESH)

    def send_raw(q, to):
        return pltpu.make_async_remote_copy(
            raw.at[q], sibling.at[q], r_send, r_recv.at[q],
            device_id={"tm": to}, device_id_type=MESH)

    def onward(q, to, sem):
        return pltpu.make_async_remote_copy(
            second.at[q], earlier.at[q], sem, c_recv.at[q],
            device_id={"tm": to}, device_id_type=MESH)

    def hand_over(q, source, parity):
        return pltpu.make_async_remote_copy(
            source.at[q], run_out.at[at(q, parity)], p_send, p_recv,
            device_id={"tm": other}, device_id_type=MESH)

    def keep_own(q, source):
        return pltpu.make_async_copy(source.at[q], run_out.at[at(q, core)], o_sem)

    def dump_send(q):
        return pltpu.make_async_remote_copy(
            second.at[q], dump_out.at[:, columns(q)], d_send, d_recv,
            device_id={"tm": (q // per_slab) * 2 + core}, device_id_type=MESH)

    def dump_keep(q):
        return pltpu.make_async_copy(second.at[q], dump_out.at[:, columns(q)], k_sem)

    def stat_copy(o):
        to = lax.rem(me + o, n)
        return pltpu.make_async_remote_copy(
            stats.at[to // share], stats_in.at[o], s_send.at[o], s_recv.at[o],
            device_id={"tm": to}, device_id_type=MESH)

    barrier = pltpu.get_barrier_semaphore()
    for o in range(1, n):
        pl.semaphore_signal(barrier, inc=1, device_id={"tm": lax.rem(me + o, n)}, device_id_type=MESH)

    opening = wide // block
    for b in range(opening):
        fetch(b).start()

    for i in range(intervals):
        keep[i : i + 1] = (antenna[i : i + 1] * channel[0, i]).astype(jnp.float32)
    stats[...] = jnp.zeros_like(stats)

    for b in range(opening):
        fetch(b).wait()

    @pl.loop(opening, blocks)
    def _(b):
        fetch(b).start()

    for b in range(opening):
        mask_block(b)
    gram_piece(0, 0)

    pl.semaphore_wait(barrier, n - 1)

    def gather(q):
        exchange(q).wait_recv()

        @pl.when(even)
        def _():
            raw[q] = gram[at(q, core)] + partner[q]
            send_raw(q, me + 2).start()

    def advance(q):
        mine = gram[at(q, core)]
        theirs = partner[q]
        low = jnp.where(core == 0, mine, theirs)
        first[q] = low

        @pl.when(chip > 1)
        def _():
            onward(q, me, c_send).wait_recv()
            first[q] = first[q] + earlier[q]

        @pl.when(jnp.logical_not(even))
        def _():
            send_raw(q, me).wait_recv()
            first[q] = first[q] + sibling[q]

        second[q] = first[q] + jnp.where(core == 0, theirs, mine)

        @pl.when(jnp.logical_not(even) & (chip < last))
        def _():
            onward(q, me + 2, c_send).start()
            onward(q, me + 4, v_send).start()

        @pl.when(chip == last)
        def _():
            @pl.when(q // per_slab < last)
            def _():
                dump_send(q).start()

            @pl.when(q // per_slab == last)
            def _():
                dump_keep(q).start()

        @pl.when(core == 0)
        def _():
            hand_over(q, second, 0).start()
            keep_own(q, first).start()

        @pl.when(core == 1)
        def _():
            hand_over(q, first, 1).start()
            keep_own(q, second).start()

    @pl.loop(0, steps + 1 + LAG)
    def _(g):
        @pl.when((g > 0) & (g < pieces))
        def _():
            for k in range(opening):
                fetch(g * opening + k).wait()
                mask_block(g * opening + k)

        @pl.when(g < steps)
        def _():
            @pl.when(g > 0)
            def _():
                gram_piece(g // pieces, g % pieces)

            for k in range(chunks):
                exchange(g * chunks + k).start()

        @pl.when((g > 0) & (g <= steps))
        def _():
            @pl.loop(0, chunks)
            def _(k):
                gather((g - 1) * chunks + k)

        due = g - 1 - lag

        @pl.when((due >= 0) & (due < steps))
        def _():
            @pl.loop(0, chunks)
            def _(k):
                advance(due * chunks + k)

        turn = g - pieces

        @pl.when((turn >= 0) & (turn < blocks))
        def _():
            moments(turn)

            @pl.when(turn == blocks - 1)
            def _():
                for o in range(1, n):
                    stat_copy(o).start()

    total = stats[me // share]
    for o in range(1, n):
        stat_copy(o).wait_recv()
        total = total + stats_in[o]
    mine = total[:, 0:rows]
    for k in range(1, share):
        mine = jnp.where(me % share == k, total[:, k * rows : (k + 1) * rows], mine)
    total = mine
    one, two, count = total[0:1], total[1:2], total[2:3]
    kurt_out[...] = (count + 1.0) / (count - 1.0) * (count * two / (one * one) - 1.0)
    for o in range(1, n):
        stat_copy(o).wait_send()

    def whole(count, send, recv):
        part = pl.ds(0, count)
        return pltpu.make_async_remote_copy(
            second.at[part], earlier.at[part], send, recv,
            device_id={"tm": other}, device_id_type=MESH)

    whole(STEPS, x_send, p_recv).wait_send()
    whole(STEPS, p_send, p_recv).wait()
    pltpu.make_async_copy(second, earlier, o_sem).wait()

    @pl.when(even)
    def _():
        whole(STEPS, r_send, p_recv).wait_send()

    @pl.when(jnp.logical_not(even) & (chip < last))
    def _():
        whole(STEPS, c_send, p_recv).wait_send()
        whole(STEPS, v_send, p_recv).wait_send()

    @pl.when(chip == last)
    def _():
        whole(STEPS - per_slab, d_send, p_recv).wait_send()
        kept = pl.ds(0, per_slab)
        pltpu.make_async_copy(second.at[kept], earlier.at[kept], k_sem).wait()

    @pl.when(chip < last)
    def _():
        whole(per_slab, d_send, d_recv).wait_recv()


def chain(volts, antenna, channel, n):
    _, signals, samples = volts.shape
    intervals = antenna.shape[0]
    rows = signals // n
    block = max(rows, 128)
    per_slab = STEPS // (n // 2)
    half = (STEPS, rows, signals // per_slab)
    dma = pltpu.SemaphoreType.DMA
    vmem = pl.BlockSpec(memory_space=pltpu.VMEM)
    hbm = pl.BlockSpec(memory_space=pl.ANY)
    return pl.pallas_call(
        functools.partial(chain_kernel, n),
        out_shape=[
            jax.ShapeDtypeStruct((signals, signals), jnp.float32),
            jax.ShapeDtypeStruct((rows, signals), jnp.float32),
            jax.ShapeDtypeStruct((1, rows), jnp.float32),
        ],
        in_specs=[
            pl.BlockSpec(memory_space=pltpu.HBM),
            vmem,
            pl.BlockSpec(memory_space=pltpu.SMEM),
        ],
        out_specs=[hbm, hbm, vmem],
        scratch_shapes=[
            pltpu.VMEM(volts.shape, volts.dtype),
            pltpu.VMEM((intervals, signals), jnp.float32),
            pltpu.VMEM((signals, signals), jnp.float32),
            pltpu.VMEM((signals // block, 8, block), jnp.float32),
            pltpu.VMEM(half, jnp.float32),
            pltpu.VMEM(half, jnp.float32),
            pltpu.VMEM(half, jnp.float32),
            pltpu.VMEM(half, jnp.float32),
            pltpu.VMEM(half, jnp.float32),
            pltpu.VMEM(half, jnp.float32),
            pltpu.VMEM((n, 8, block), jnp.float32),
            dma((signals // block,)),
            dma, dma((STEPS,)), dma, dma((STEPS,)), dma, dma, dma((STEPS,)),
            dma, dma, dma, dma, dma, dma,
            dma((n,)), dma((n,)),
        ],
        compiler_params=pltpu.CompilerParams(
            collective_id=0, has_side_effects=True, vmem_limit_bytes=VMEM_BYTES
        ),
    )(volts, antenna, channel)


def per_device(voltages, antenna_flags, channel_flags):
    n = lax.axis_size("tm")
    running, dump_rows, kurtosis = chain(
        voltages[0], antenna_flags[0], channel_flags, n
    )
    return (running[None, None], dump_rows[None], kurtosis)


def solution(mesh):
    return jax.shard_map(
        per_device,
        mesh=mesh,
        in_specs=(P("band", None, None, "tm"), P("band", "tm", None), P("band", "tm")),
        out_specs=(P("band", "tm", None, None), P("band", "tm", None), P("band", "tm")),
        check_vma=False,
    )
```
